32 devices in a mesh: dp: 8 (over z, x), mp: 4 (over y, core).
Axes of the slice: x: 2, y: 2, z: 4, core: 2. Of those that a mesh axis runs over, the one named last changes fastest.
Arguments:
- acts: bfloat16 [2048, 8192], P('dp'), may hold values from -6 to 6
- cotangent: bfloat16 [2048, 8192], P('dp', 'mp'), may hold values from -1.25 to 1.25
- basis: float32 [8192, 512], P('dp'), may hold values from -0.0625 to 0.0625
- tangent: float32 [8192, 512], P('dp'), may hold values from -0.0625 to 0.0625
- rotation: float32 [512, 512], replicated, may hold values from -0.25 to 0.25
- angles: float32 [512], replicated, may hold values from 0 to 1.2
- first_moment: float32 [512, 8192], P('dp', 'mp'), may hold values from -6 to 6
- second_moment: float32 [512, 8192], P('dp', 'mp'), may hold values from 0.25 to 4
Outputs:
- update: float32 [8192, 8192], P('dp', 'mp')
- new_basis: float32 [8192, 512], P('dp')
- new_first: float32 [512, 8192], P('dp', 'mp')
- new_second: float32 [512, 8192], P('dp', 'mp')
The draws below stay inside these ranges and needn't reach their ends.
All inputs are finite; a program needn't handle non-finite values.
Results may differ from the reference program's by a relative error of at most 0.0006.
The reference program's roundings to bfloat16 on the way (of `basis_half`, `projected` and `direction`) count: a program that leaves them out, or rounds other values in their place, can miss the bound.
Values may be sent and summed in bfloat16 or wider, within the bound.
No kernel may reach another device: no remote copies, remote signals or barrier semaphores. Data moves between devices by JAX's collectives and lax.ppermute only.
A program may use at most 128 MiB of HBM per device.

```python
import math
import jax
import jax.numpy as jnp
from jax import lax

D = 8192
R = 512
TOKENS = 2048


def steps_of(key, shape, cuts, low, high):
    level, own = 1.0, jax.random.fold_in(key, 6)
    for dim, blocks in cuts:
        draws = jnp.exp(jax.random.uniform(jax.random.fold_in(own, dim), (blocks,), jnp.float32, low / len(cuts), high / len(cuts)))
        level = level * jnp.repeat(draws, shape[dim] // blocks).reshape([-1 if axis == dim else 1 for axis in range(len(shape))])
    return level


def scatter_about(own_key, dims, scale, bound, shards=(), kind=jnp.bfloat16):
    drawn = jax.random.normal(own_key, dims, jnp.float32) * scale
    if len(shards) > 0:
        drawn = steps_of(own_key, dims, shards, -0.22, 0.18) * drawn
    return jnp.clip(drawn, min=-bound, max=bound).astype(kind)


def setup_inputs(seed: int = 0) -> dict:
    key_of = jax.random.split(jax.random.key(seed), 9)
    acts = scatter_about(key_of[0], (TOKENS, D), 1.0, 6.0, ((0, 8),))
    cotangent = scatter_about(key_of[1], (TOKENS, D), (4.0 / (TOKENS ** 0.5)), 1.25, ((0, 8), (1, 4)))
    basis = scatter_about(key_of[2], (D, R), D ** -0.5, 0.0625, ((0, 8),), jnp.float32)
    tangent = scatter_about(key_of[3], (D, R), D ** -0.5, 0.0625, ((0, 8),), jnp.float32)
    rotation = scatter_about(key_of[4], (R, R), R ** -0.5, 0.25, (), jnp.float32)
    angles = jnp.clip(jax.random.uniform(key_of[5], (R,), jnp.float32, 0.0, 1.2), 0.0, 1.2)
    first_moment = scatter_about(key_of[6], (R, D), 1.0, 6.0, ((0, 8), (1, 4)), jnp.float32)
    second_moment = jnp.clip(jnp.exp(math.log(4.0) - 2.7725887 * jax.random.uniform(key_of[7], (R, D), jnp.float32) ** steps_of(key_of[7], (R, D), ((0, 8), (1, 4)), -0.2, 0.2)), 0.25, 4.0)
    return dict(acts=acts, cotangent=cotangent, basis=basis, tangent=tangent, rotation=rotation, angles=angles, first_moment=first_moment, second_moment=second_moment)


def reference(acts, cotangent, basis, tangent, rotation, angles, first_moment, second_moment):
    highest = lax.Precision.HIGHEST
    basis_half = basis.astype(jnp.bfloat16)
    projected = jnp.dot(acts, basis_half, preferred_element_type=jnp.float32).astype(jnp.bfloat16)
    grad = lax.dot_general(projected, cotangent, (((0,), (0,)), ((), ())), preferred_element_type=jnp.float32)
    rms = jnp.sqrt(jnp.mean(grad * grad) + 1e-06)
    clipped = grad * jnp.minimum(1.0, 1.0 / rms)
    moment_a = 0.9 * first_moment + 0.1 * clipped
    moment_b = 0.999 * second_moment + 0.001 * clipped * clipped
    bias_a = 1.0 - 0.9 ** 10
    bias_b = 1.0 - 0.999 ** 10
    direction = (moment_a / bias_a / (jnp.sqrt(moment_b / bias_b) + 1e-08)).astype(jnp.bfloat16)
    update = jnp.dot(basis_half, direction, preferred_element_type=jnp.float32)
    turned = jnp.dot(basis, rotation, precision=highest)
    mixed = turned * (jnp.cos(angles) - 1.0) + tangent * jnp.sin(angles)
    new_basis = basis + jnp.dot(mixed, rotation.T, precision=highest)
    intersection = jnp.dot(new_basis.T, basis, precision=highest)
    new_first = jnp.dot(intersection, moment_a, precision=highest)
    new_second = jnp.dot(intersection * intersection, moment_b, precision=highest)
    return (update, new_basis, new_first, new_second)
```

```python
import jax
import jax.numpy as jnp
from jax import lax
from jax.sharding import PartitionSpec as P

D = 8192
R = 512
HOPS = 8


def hop(x, axis, step):
    size = lax.axis_size(axis)
    return lax.ppermute(x, axis, [(i, i ^ step) for i in range(size)])


def gather_xor(x, axis):
    size = lax.axis_size(axis)
    me = lax.axis_index(axis)
    if size > HOPS:
        every = lax.all_gather(x, axis)
        return [lax.dynamic_index_in_dim(every, me ^ s, 0, keepdims=False) for s in range(size)]
    blocks = {0: x}
    step = size // 2
    while step:
        for s in sorted(blocks):
            blocks[s ^ step] = hop(blocks[s], axis, step)
        step //= 2
    return [blocks[s] for s in range(size)]


def exchange_xor(piece, axis):
    size = lax.axis_size(axis)
    me = lax.axis_index(axis)
    if size > HOPS:
        every = lax.all_to_all(jnp.stack([piece(d) for d in range(size)]), axis, 0, 0)
        return [lax.dynamic_index_in_dim(every, me ^ s, 0, keepdims=False) for s in range(size)]
    got = [piece(me)]
    for s in range(1, size):
        got.append(hop(piece(me ^ s), axis, s))
    return got


def total_xor(x, axis):
    step = 1
    while step < lax.axis_size(axis):
        x = x + hop(x, axis, step)
        step *= 2
    return x


def local(acts, cotangent, basis, tangent, rotation, angles, first_moment, second_moment):
    highest = lax.Precision.HIGHEST
    f32 = jnp.float32
    dp, mp = lax.axis_size("dp"), lax.axis_size("mp")
    me, col = lax.axis_index("dp"), lax.axis_index("mp")
    rows, rank = basis.shape
    own_rows, width = first_moment.shape
    part = rank // mp
    block = width // dp

    basis_half = basis.astype(jnp.bfloat16)
    own_half = lax.dynamic_slice(basis_half, (0, col * part), (rows, part))
    gathered = gather_xor(own_half, "dp")
    projected = sum(
        jnp.dot(
            lax.dynamic_slice(acts, (0, (me ^ s) * rows), (acts.shape[0], rows)),
            gathered[s],
            preferred_element_type=f32,
        )
        for s in range(dp)
    ).astype(jnp.bfloat16)

    tokens = exchange_xor(
        lambda d: lax.dynamic_slice(cotangent, (0, d * block), (cotangent.shape[0], block)), "dp"
    )
    cot = jnp.concatenate(tokens, axis=0)

    mine = jnp.concatenate(gather_xor(projected, "dp"), axis=0)
    proj = jnp.concatenate(gather_xor(mine, "mp"), axis=1)
    grad = lax.dot_general(proj, cot, (((0,), (0,)), ((), ())), preferred_element_type=f32)

    both = jnp.stack([first_moment, second_moment])
    moved = exchange_xor(
        lambda d: lax.dynamic_slice(both, (0, 0, d * block), (2, own_rows, block)), "dp"
    )
    moved = jnp.stack(moved)
    per = dp // mp
    order = [(col ^ (p // per)) * per + p % per for p in range(dp)]
    moved = jnp.concatenate(
        [lax.dynamic_index_in_dim(moved, me ^ k, 0, keepdims=False) for k in order], axis=1
    )

    squares = jnp.sum((grad * grad).reshape(-1, 8, block), axis=0)
    squares = jnp.sum(total_xor(total_xor(squares, "mp"), "dp"))
    rms = jnp.sqrt(squares / (R * D) + 1e-06)
    clipped = grad * jnp.minimum(1.0, 1.0 / rms)
    moment_a = 0.9 * moved[0] + 0.1 * clipped
    moment_b = 0.999 * moved[1] + 0.001 * clipped * clipped
    bias_a = 1.0 - 0.9**10
    bias_b = 1.0 - 0.999**10
    direction = (moment_a / bias_a / (jnp.sqrt(moment_b / bias_b) + 1e-08)).astype(jnp.bfloat16)

    directions = gather_xor(direction, "dp")
    turned_half = jnp.concatenate(
        [lax.dynamic_slice(basis_half, (0, (col ^ t) * part), (rows, part)) for t in range(mp)],
        axis=1,
    )
    stacked = jnp.stack(directions)
    whole = jnp.concatenate(
        [lax.dynamic_index_in_dim(stacked, me ^ k, 0, keepdims=False) for k in range(dp)], axis=1
    )
    update = jnp.dot(turned_half, whole, preferred_element_type=f32)

    turned = jnp.dot(basis, rotation, precision=highest)
    mixed = turned * (jnp.cos(angles) - 1.0) + tangent * jnp.sin(angles)
    new_basis = basis + jnp.dot(mixed, rotation.T, precision=highest)
    own_basis = lax.dynamic_slice(basis, (0, col * part), (rows, part))
    inter = jnp.dot(new_basis.T, own_basis, precision=highest)
    inter = total_xor(inter, "dp")
    inter = jnp.concatenate(gather_xor(inter, "mp"), axis=1)

    new_a = jnp.dot(inter, moment_a, precision=highest)
    new_b = jnp.dot(inter * inter, moment_b, precision=highest)
    new = jnp.stack([new_a, new_b])
    back = jnp.stack(
        exchange_xor(
            lambda d: lax.dynamic_slice(new, (0, d * own_rows, 0), (2, own_rows, block)), "dp"
        )
    )
    back = jnp.concatenate(
        [lax.dynamic_index_in_dim(back, me ^ k, 0, keepdims=False) for k in range(dp)], axis=2
    )
    return (update, new_basis, back[0], back[1])


def solution(mesh):
    in_specs = (
        P("dp", None),
        P("dp", "mp"),
        P("dp", None),
        P("dp", None),
        P(),
        P(),
        P("dp", "mp"),
        P("dp", "mp"),
    )
    out_specs = (P("dp", "mp"), P("dp", None), P("dp", "mp"), P("dp", "mp"))
    return jax.shard_map(local, mesh=mesh, in_specs=in_specs, out_specs=out_specs, check_vma=False)
```

```python
import functools

import jax
import jax.numpy as jnp
from jax import lax
from jax.experimental import pallas as pl
from jax.experimental.pallas import tpu as pltpu
from jax.sharding import PartitionSpec as P

D = 8192
R = 512
HOPS = 8


def hop(x, axis, step):
    size = lax.axis_size(axis)
    return lax.ppermute(x, axis, [(i, i ^ step) for i in range(size)])


def gather_xor(x, axis):
    size = lax.axis_size(axis)
    me = lax.axis_index(axis)
    if size > HOPS:
        every = lax.all_gather(x, axis)
        return [lax.dynamic_index_in_dim(every, me ^ s, 0, keepdims=False) for s in range(size)]
    blocks = {0: x}
    step = size // 2
    while step:
        for s in sorted(blocks):
            blocks[s ^ step] = hop(blocks[s], axis, step)
        step //= 2
    return [blocks[s] for s in range(size)]


def exchange(x, axis):
    return lax.all_to_all(x, axis, 0, 0)


def total_xor(x, axis):
    step = 1
    while step < lax.axis_size(axis):
        x = x + hop(x, axis, step)
        step *= 2
    return x


def columns_by_owner(x, count):
    rows, width = x.shape
    return x.reshape(rows, count, width // count).transpose(1, 0, 2)


def after(x, *others):
    return lax.optimization_barrier((x,) + others)[0]


def reorder_kernel(me_ref, x_ref, out_ref):
    out_ref[...] = x_ref[...]


def reorder(x, me):
    count, rows, width = x.shape
    spec = lambda index: pl.BlockSpec((1, rows, width), index)
    return pl.pallas_call(
        reorder_kernel,
        out_shape=jax.ShapeDtypeStruct(x.shape, x.dtype),
        grid_spec=pltpu.PrefetchScalarGridSpec(
            num_scalar_prefetch=1,
            grid=(count,),
            in_specs=[spec(lambda s, me_ref: (me_ref[0] ^ s, 0, 0))],
            out_specs=spec(lambda s, me_ref: (s, 0, 0)),
        ),
        cost_estimate=pl.CostEstimate(
            flops=0, bytes_accessed=2 * x.size * x.dtype.itemsize, transcendentals=0
        ),
        name="reorder",
    )(me.reshape(1), x)


def adam_kernel(count, col_ref, moved_ref, *refs):
    grads, (squares_ref, a_ref, b_ref, direction_ref) = refs[:-4], refs[-4:]
    blocks, rows = moved_ref.shape[0], moved_ref.shape[1] // 2
    per = blocks // mp_of(grads)
    squares = jnp.sum(squares_ref[...])
    rms = jnp.sqrt(squares / count + 1e-06)
    scale = jnp.minimum(1.0, 1.0 / rms)
    bias_a = 1.0 - 0.9**10
    bias_b = 1.0 - 0.999**10
    for t, grad_ref in enumerate(grads):
        for h in range(per):
            k = (col_ref[0] ^ t) * per + h
            at = (t * per + h) * rows
            clipped = grad_ref[h * rows : (h + 1) * rows, :] * scale
            moment_a = 0.9 * moved_ref[k, :rows, :] + 0.1 * clipped
            moment_b = 0.999 * moved_ref[k, rows:, :] + 0.001 * clipped * clipped
            a_ref[at : at + rows, :] = moment_a
            b_ref[at : at + rows, :] = moment_b
            direction = moment_a / bias_a / (jnp.sqrt(moment_b / bias_b) + 1e-08)
            direction_ref[at : at + rows, :] = direction.astype(direction_ref.dtype)


def mp_of(grads):
    return len(grads)


def adam(moved, grads, squares, col, count):
    rank = moved.shape[0] * moved.shape[1] // 2
    block = moved.shape[2]
    out = lambda dtype: jax.ShapeDtypeStruct((rank, block), dtype)
    vmem = pl.BlockSpec(memory_space=pltpu.VMEM)
    return pl.pallas_call(
        functools.partial(adam_kernel, float(count)),
        out_shape=(out(jnp.float32), out(jnp.float32), out(jnp.bfloat16)),
        in_specs=[pl.BlockSpec(memory_space=pltpu.SMEM)] + [vmem] * (2 + len(grads)),
        out_specs=(vmem, vmem, vmem),
        cost_estimate=pl.CostEstimate(
            flops=20 * rank * block, bytes_accessed=22 * rank * block, transcendentals=rank * block
        ),
        name="adam",
    )(col.reshape(1), moved, *grads, squares)


def update_kernel(place_ref, half_ref, block_ref, *refs):
    out_ref = refs[-1]
    out_ref[...] = jnp.dot(half_ref[...], block_ref[0], preferred_element_type=jnp.float32)


def update_part(half, blocks, places, width, into):
    rows, rank = half.shape
    count, _, block = blocks.shape
    tile = rows // 2 if rows % 32 == 0 else rows
    specs = [
        pl.BlockSpec((tile, rank), lambda n, r, place: (r, 0)),
        pl.BlockSpec((1, rank, block), lambda n, r, place: (n, 0, 0)),
    ]
    operands = [half, blocks]
    alias = {}
    if into is not None:
        specs.append(pl.BlockSpec(memory_space=pl.ANY))
        operands.append(into)
        alias = {3: 0}
    return pl.pallas_call(
        update_kernel,
        out_shape=jax.ShapeDtypeStruct((rows, width), jnp.float32),
        grid_spec=pltpu.PrefetchScalarGridSpec(
            num_scalar_prefetch=1,
            grid=(count, rows // tile),
            in_specs=specs,
            out_specs=pl.BlockSpec((tile, block), lambda n, r, place: (r, place[n])),
        ),
        input_output_aliases=alias,
        cost_estimate=pl.CostEstimate(
            flops=2 * rows * rank * block * count,
            bytes_accessed=4 * rows * block * count,
            transcendentals=0,
        ),
        name="update",
    )(places, *operands)


def local(acts, cotangent, basis, tangent, rotation, angles, first_moment, second_moment):
    highest = lax.Precision.HIGHEST
    f32 = jnp.float32
    dp, mp = lax.axis_size("dp"), lax.axis_size("mp")
    me, col = lax.axis_index("dp"), lax.axis_index("mp")
    rows, rank = basis.shape
    own_rows, width = first_moment.shape
    part = rank // mp
    block = width // dp

    own_basis = lax.dynamic_slice(basis, (0, col * part), (rows, part))
    gathered = gather_xor(own_basis.astype(jnp.bfloat16), "dp")
    projected = sum(
        jnp.dot(
            lax.dynamic_slice(acts, (0, (me ^ s) * rows), (acts.shape[0], rows)),
            gathered[s],
            preferred_element_type=f32,
        )
        for s in range(dp)
    ).astype(jnp.bfloat16)

    cot = reorder(exchange(columns_by_owner(cotangent, dp), "dp"), me).reshape(-1, block)
    cot_across = hop(cot, "mp", 2)

    both = jnp.concatenate([first_moment, second_moment], axis=0)
    both = after(columns_by_owner(both, dp), cot[:8])
    moved = exchange(both, "dp")

    mine = jnp.concatenate(gather_xor(projected, "dp"), axis=0)
    grads, across, squares = [], [], 0.0
    for proj in (mine, hop(mine, "mp", 1)):
        for cols, kept in ((cot, grads), (cot_across, across)):
            grad = lax.dot_general(proj, cols, (((0,), (0,)), ((), ())), preferred_element_type=f32)
            kept.append(grad)
            squares = squares + jnp.sum((grad * grad).reshape(-1, 8, block), axis=0)
    across = hop(jnp.concatenate(across, axis=0), "mp", 2)
    grads = grads + [across[:part], across[part:]]

    squares = jnp.sum(squares.reshape(8, -1, 128) if block % 128 == 0 else squares[:, None], axis=1)
    squares = jnp.broadcast_to(squares, (dp * mp,) + squares.shape)
    squares = exchange(squares, ("dp", "mp"))
    moment_a, moment_b, direction = adam(moved, grads, squares, col, R * D)

    basis_half = basis.astype(jnp.bfloat16)
    turned_half = jnp.concatenate(
        [lax.dynamic_slice(basis_half, (0, (col ^ t) * part), (rows, part)) for t in range(mp)],
        axis=1,
    )
    directions = gather_xor(direction, "dp")
    if block % 128 == 0:
        update = None
        for group in ([s for s in range(dp) if s % 2 == 0], [s for s in range(dp) if s % 2]):
            update = update_part(
                turned_half,
                jnp.stack([directions[s] for s in group]),
                jnp.stack([me ^ s for s in group]),
                width,
                update,
            )
    else:
        stacked = jnp.stack(directions)
        whole = jnp.concatenate(
            [lax.dynamic_index_in_dim(stacked, me ^ k, 0, keepdims=False) for k in range(dp)],
            axis=1,
        )
        update = jnp.dot(turned_half, whole, preferred_element_type=f32)

    turned = jnp.dot(basis, rotation, precision=highest)
    mixed = turned * (jnp.cos(angles) - 1.0) + tangent * jnp.sin(angles)
    new_basis = basis + jnp.dot(mixed, rotation.T, precision=highest)
    inter = jnp.dot(new_basis.T, own_basis, precision=highest)
    inter = total_xor(inter, "dp")
    inter = jnp.concatenate(gather_xor(inter, "mp"), axis=1)

    new_a = jnp.dot(inter, moment_a, precision=highest).reshape(dp, own_rows, block)
    new_b = jnp.dot(inter * inter, moment_b, precision=highest).reshape(dp, own_rows, block)
    back = exchange(jnp.concatenate([new_a, new_b], axis=1), "dp")
    back = back.transpose(1, 0, 2).reshape(2 * own_rows, width)
    return (update, new_basis, back[:own_rows], back[own_rows:])


def solution(mesh):
    in_specs = (
        P("dp", None),
        P("dp", "mp"),
        P("dp", None),
        P("dp", None),
        P(),
        P(),
        P("dp", "mp"),
        P("dp", "mp"),
    )
    out_specs = (P("dp", "mp"), P("dp", None), P("dp", "mp"), P("dp", "mp"))
    return jax.shard_map(local, mesh=mesh, in_specs=in_specs, out_specs=out_specs, check_vma=False)
```

```python
import functools

import jax
import jax.numpy as jnp
from jax import lax
from jax.experimental import pallas as pl
from jax.experimental.pallas import tpu as pltpu
from jax.sharding import PartitionSpec as P

D = 8192
R = 512
HOPS = 8


VMEM = pl.BlockSpec(memory_space=pltpu.VMEM)
SMEM = pl.BlockSpec(memory_space=pltpu.SMEM)
ANY = pl.BlockSpec(memory_space=pl.ANY)


def hop(x, axis, step):
    size = lax.axis_size(axis)
    return lax.ppermute(x, axis, [(i, i ^ step) for i in range(size)])


def gather_xor(x, axis):
    size = lax.axis_size(axis)
    me = lax.axis_index(axis)
    if size > HOPS:
        every = lax.all_gather(x, axis)
        return [lax.dynamic_index_in_dim(every, me ^ s, 0, keepdims=False) for s in range(size)]
    blocks = {0: x}
    step = size // 2
    while step:
        for s in sorted(blocks):
            blocks[s ^ step] = hop(blocks[s], axis, step)
        step //= 2
    return [blocks[s] for s in range(size)]


def total_xor(x, axis):
    step = 1
    while step < lax.axis_size(axis):
        x = x + hop(x, axis, step)
        step *= 2
    return x


def exchange(x, axis):
    return lax.all_to_all(x, axis, 0, 0)


def place(blocks, me):
    out = jnp.zeros((len(blocks),) + blocks[0].shape, blocks[0].dtype)
    for s, x in enumerate(blocks):
        out = lax.dynamic_update_slice(out, x[None], (me ^ s,) + (0,) * x.ndim)
    return out


def whole_call(kernel, out_shape, operands, scalars=(), flops=0):
    outs = jax.tree.leaves(out_shape)
    moved = sum(math_size(x) for x in list(operands) + outs)
    return pl.pallas_call(
        kernel,
        out_shape=out_shape,
        in_specs=[SMEM] * len(scalars) + [VMEM] * len(operands),
        out_specs=jax.tree.map(lambda _: VMEM, out_shape),
        cost_estimate=pl.CostEstimate(flops=flops, bytes_accessed=moved, transcendentals=0),
    )(*[x.reshape(1) for x in scalars], *operands)


def math_size(x):
    return x.size * jnp.dtype(x.dtype).itemsize


def pack_kernel(*refs):
    *ins, out_ref = refs
    block = out_ref.shape[2]
    at = 0
    for x_ref in ins:
        rows = x_ref.shape[0]
        for k in range(out_ref.shape[0]):
            out_ref[k, at : at + rows, :] = x_ref[:, k * block : (k + 1) * block]
        at += rows


def by_owner(arrays, count):
    width = arrays[0].shape[1]
    if (width // count) % 128:
        x = jnp.concatenate(arrays, axis=0)
        return x.reshape(-1, count, width // count).transpose(1, 0, 2)
    rows = sum(x.shape[0] for x in arrays)
    out = jax.ShapeDtypeStruct((count, rows, width // count), arrays[0].dtype)
    return whole_call(pack_kernel, out, arrays)


def unpack_kernel(x_ref, *outs):
    block = x_ref.shape[2]
    at = 0
    for out_ref in outs:
        rows = out_ref.shape[0]
        for k in range(x_ref.shape[0]):
            out_ref[:, k * block : (k + 1) * block] = x_ref[k, at : at + rows, :]
        at += rows


def from_owner(x, pieces):
    count, rows, block = x.shape
    rows //= pieces
    if block % 128:
        x = x.transpose(1, 0, 2).reshape(pieces, rows, count * block)
        return tuple(x[i] for i in range(pieces))
    out = jax.ShapeDtypeStruct((rows, count * block), x.dtype)
    return whole_call(unpack_kernel, (out,) * pieces, [x])


def adam_kernel(count, col_ref, moved_ref, *refs):
    grads, (squares_ref, a_ref, b_ref, direction_ref) = refs[:-4], refs[-4:]
    rows = moved_ref.shape[1] // 2
    squares = jnp.sum(squares_ref[...])
    rms = jnp.sqrt(squares / count + 1e-06)
    scale = jnp.minimum(1.0, 1.0 / rms)
    bias_a = 1.0 - 0.9**10
    bias_b = 1.0 - 0.999**10
    ranks = sum(grad_ref.shape[0] for grad_ref in grads) // rows
    per = ranks // 4
    at = 0
    for grad_ref in grads:
        for h in range(grad_ref.shape[0] // rows):
            n = at // rows
            k = (col_ref[0] ^ (n // per)) * per + n % per
            clipped = grad_ref[h * rows : (h + 1) * rows, :] * scale
            moment_a = 0.9 * moved_ref[k, :rows, :] + 0.1 * clipped
            moment_b = 0.999 * moved_ref[k, rows:, :] + 0.001 * clipped * clipped
            a_ref[at : at + rows, :] = moment_a
            b_ref[at : at + rows, :] = moment_b
            direction = moment_a / bias_a / (jnp.sqrt(moment_b / bias_b) + 1e-08)
            direction_ref[at : at + rows, :] = direction.astype(direction_ref.dtype)
            at += rows


def adam(moved, grads, squares, col, count):
    rank = moved.shape[0] * moved.shape[1] // 2
    block = moved.shape[2]
    out = lambda dtype: jax.ShapeDtypeStruct((rank, block), dtype)
    return whole_call(
        functools.partial(adam_kernel, float(count)),
        (out(jnp.float32), out(jnp.float32), out(jnp.bfloat16)),
        [moved, *grads, squares],
        scalars=[col],
    )


def update_kernel(group, me_ref, half_ref, *refs):
    blocks, (out_ref, done_ref, sem) = refs[: len(group)], refs[-3:]
    block = blocks[0].shape[1]
    copies = []
    for n, block_ref in enumerate(blocks):
        done_ref[n] = jnp.dot(half_ref[...], block_ref[...], preferred_element_type=jnp.float32)
        at = pl.multiple_of((me_ref[0] ^ group[n]) * block, block)
        copies.append(
            pltpu.make_async_copy(done_ref.at[n], out_ref.at[:, pl.ds(at, block)], sem.at[n])
        )
        copies[-1].start()
    for copy in copies:
        copy.wait()


def update_part(half, blocks, group, me, width, into):
    rows, rank = half.shape
    block = blocks[0].shape[1]
    count = len(blocks)
    more = [] if into is None else [into]
    return pl.pallas_call(
        functools.partial(update_kernel, group),
        out_shape=jax.ShapeDtypeStruct((rows, width), jnp.float32),
        in_specs=[SMEM, VMEM] + [VMEM] * count + [ANY] * len(more),
        out_specs=ANY,
        scratch_shapes=[
            pltpu.VMEM((count, rows, block), jnp.float32),
            pltpu.SemaphoreType.DMA((count,)),
        ],
        input_output_aliases={2 + count: 0} if more else {},
        cost_estimate=pl.CostEstimate(
            flops=2 * rows * rank * block * count,
            bytes_accessed=4 * rows * block * count,
            transcendentals=0,
        ),
        name="update",
    )(me.reshape(1), half, *blocks, *more)


def step(acts, cotangent, basis, tangent, rotation, angles, first_moment, second_moment):
    highest = lax.Precision.HIGHEST
    f32 = jnp.float32
    dp, mp = lax.axis_size("dp"), lax.axis_size("mp")
    me, col = lax.axis_index("dp"), lax.axis_index("mp")
    rows, rank = basis.shape
    own_rows, width = first_moment.shape
    part = rank // mp
    block = width // dp

    own_basis = lax.dynamic_slice(basis, (0, col * part), (rows, part))
    gathered = gather_xor(own_basis.astype(jnp.bfloat16), "dp")
    projected = sum(
        jnp.dot(
            lax.dynamic_slice(acts, (0, (me ^ s) * rows), (acts.shape[0], rows)),
            gathered[s],
            preferred_element_type=f32,
        )
        for s in range(dp)
    ).astype(jnp.bfloat16)

    cot = by_owner([cotangent], dp)
    cot = exchange(cot, "dp").reshape(-1, block)
    cot_across = hop(cot, "mp", 2)

    both = by_owner([first_moment, second_moment], dp)
    moved = exchange(both, "dp")

    mine = gather_xor(projected, "dp")
    mine = place(mine, me).reshape(-1, part)
    other = hop(mine, "mp", 1)
    grads, across, squares = [], [], 0.0
    for proj in (mine, other):
        for cols, kept in ((cot, grads), (cot_across, across)):
            grad = lax.dot_general(proj, cols, (((0,), (0,)), ((), ())), preferred_element_type=f32)
            kept.append(grad)
            squares = squares + jnp.sum((grad * grad).reshape(-1, 8, block), axis=0)
    across = hop(jnp.concatenate(across, axis=0), "mp", 2)
    if block % 128 == 0:
        squares = jnp.sum(squares.reshape(8, -1, 128), axis=1)
    squares = jnp.broadcast_to(squares, (dp * mp,) + squares.shape)
    squares = exchange(squares, ("dp", "mp"))
    moment_a, moment_b, direction = adam(moved, grads + [across], squares, col, R * D)

    half = jnp.concatenate(
        [lax.dynamic_slice(basis, (0, (col ^ t) * part), (rows, part)) for t in range(mp)],
        axis=1,
    ).astype(jnp.bfloat16)
    directions = gather_xor(direction, "dp")
    if block % 128 == 0:
        update = None
        for group in ([s for s in range(dp) if s % 2 == 0], [s for s in range(dp) if s % 2]):
            update = update_part(
                half,
                [directions[s] for s in group],
                group,
                me,
                width,
                update,
            )
    else:
        whole = place(directions, me).transpose(1, 0, 2).reshape(rank, width)
        update = jnp.dot(half, whole, preferred_element_type=f32)

    basis, _ = lax.optimization_barrier((basis, gathered[0]))
    own_basis = lax.dynamic_slice(basis, (0, col * part), (rows, part))
    turned = jnp.dot(basis, rotation, precision=highest)
    mixed = turned * (jnp.cos(angles) - 1.0) + tangent * jnp.sin(angles)
    new_basis = basis + jnp.dot(mixed, rotation.T, precision=highest)
    inter = jnp.dot(new_basis.T, own_basis, precision=highest)
    inter = total_xor(inter, "dp")
    inter = jnp.concatenate(gather_xor(inter, "mp"), axis=1)

    new_a = jnp.dot(inter, moment_a, precision=highest).reshape(dp, own_rows, block)
    new_b = jnp.dot(inter * inter, moment_b, precision=highest).reshape(dp, own_rows, block)
    back = jnp.concatenate([new_a, new_b], axis=1)
    back = exchange(back, "dp")
    new_first, new_second = from_owner(back, 2)
    return (update, new_basis, new_first, new_second)


def solution(mesh):
    in_specs = (
        P("dp", None),
        P("dp", "mp"),
        P("dp", None),
        P("dp", None),
        P(),
        P(),
        P("dp", "mp"),
        P("dp", "mp"),
    )
    out_specs = (P("dp", "mp"), P("dp", None), P("dp", "mp"), P("dp", "mp"))
    return jax.shard_map(step, mesh=mesh, in_specs=in_specs, out_specs=out_specs, check_vma=False)
```
